256 devices in a mesh: feat: 32 (over y, x, z_hi), lane: 8 (over z_lo, core).
Axes of the slice: x: 4, y: 4, z: 8 (z_hi: 2, z_lo: 4; z = z_hi * 4 + z_lo), core: 2. Of those that a mesh axis runs over, the one named last changes fastest.
Arguments:
- activations: bfloat16 [16384, 16384], P('lane', 'feat'), may hold values from -6 to 6
- out_grads: bfloat16 [16384, 16384], P('lane', 'feat'), may hold values from -6 to 6
- project_in: bfloat16 [16384, 32], P('feat'), may hold values from -0.046875 to 0.046875
- project_out: bfloat16 [16384, 64], P('feat'), may hold values from -0.046875 to 0.046875
- lengths: int32 [512], P('lane'), may hold values from 1 to 32, 10240 in all
- stored_grads: bfloat16 [393216, 2048], P(('feat', 'lane')), may hold values from -0.125 to 0.125
Outputs:
- scores: bfloat16 [512, 393216], P(None, ('feat', 'lane'))
The draws below stay inside these ranges and needn't reach their ends.
Inputs may be any that keep to these rules, and one draw needn't show every extreme that they name: lengths sum to 10240 and one of them is exactly 32; a query's live slots come first.
All inputs are finite; a program needn't handle non-finite values. No bound on the sum of `lengths` on one device may be relied on, other than what follows from the above.
Results may differ from the reference program's by a relative error of at most 0.0064.
Values may be sent and summed in bfloat16 or wider, within the bound.
No kernel may reach another device: no remote copies, remote signals or barrier semaphores. Data moves between devices by JAX's collectives and lax.ppermute only.
A program may use at most 64 MiB of HBM per device.

```python
import math
import jax
import jax.numpy as jnp
import numpy as np
from jax import lax

D = 16384
RA = 32
RG = 64
GW = 2048
SLOTS = 32
STORE_DEV = 1536
QUERIES = 512
TOKENS = 16384
STORE = 393216


def level_of(rng, dims, shards, low, top_value):
    loudness, own = 1.0, jax.random.fold_in(rng, 6)
    for dim, shards_of in shards:
        draws = jnp.exp(jax.random.uniform(jax.random.fold_in(own, dim), (shards_of,), jnp.float32, low / len(shards), top_value / len(shards)))
        loudness = loudness * jnp.repeat(draws, dims[dim] // shards_of).reshape([-1 if axis == dim else 1 for axis in range(len(dims))])
    return loudness


def length_profile(amount, total, bound, lean):
    loads = [(1 << 20) // math.isqrt(rank ** lean) + 1 for rank in range(2, amount + 1)]
    surplus, holding = total - bound - (amount - 1), [1] * (amount - 1)
    while surplus > 0:
        free = [i for i in range(amount - 1) if holding[i] < bound]
        whole, budget = sum([loads[i] for i in free]), surplus
        for i in free:
            addition = min(bound - holding[i], max(1, budget * loads[i] // whole), surplus)
            holding[i] = holding[i] + addition
            surplus = surplus - addition
    return np.array([bound] + holding)


def ragged_sizes(stream_key, number_of, total, bound, lean):
    if number_of == 2:
        one = jax.random.randint(stream_key, (), max(1, total - bound), min(bound, total - 1) + 1)
        return jnp.stack([one, total - one])
    sizes = jnp.asarray(length_profile(number_of, total, bound, lean), jnp.int32)
    couples = (number_of - 1) // 2
    donor, receiver = sizes[1:1 + 2 * couples:2], sizes[2:2 + 2 * couples:2]
    room = jnp.minimum(donor - 1, bound - receiver)
    moved = jax.random.randint(jax.random.fold_in(stream_key, 1), (couples,), 0, 1 << 20) % (room + 1)
    sizes = sizes.at[1:1 + 2 * couples:2].set(donor - moved).at[2:2 + 2 * couples:2].set(receiver + moved)
    return sizes[jax.random.permutation(jax.random.fold_in(stream_key, 2), number_of)]


def normal_values(key, dims, deviation, bound, cuts=(), kind=jnp.bfloat16):
    entries = jax.random.normal(key, dims, jnp.float32) * deviation
    if len(cuts) > 0:
        entries = level_of(key, dims, cuts, -0.22, 0.18) * entries
    return jnp.clip(entries, min=-bound, max=bound).astype(kind)


def setup_inputs(seed: int = 0) -> dict:
    splits = jax.random.split(jax.random.key(seed), 7)
    activations = normal_values(splits[0], (TOKENS, D), 1.0, 6.0, ((0, 8), (1, 32)))
    out_grads = normal_values(splits[1], (TOKENS, D), 1.0, 6.0, ((0, 8), (1, 32)))
    project_in = normal_values(splits[2], (D, RA), D ** -0.5, 0.046875, ((0, 32),))
    project_out = normal_values(splits[3], (D, RG), D ** -0.5, 0.046875, ((0, 32),))
    lengths = ragged_sizes(splits[4], QUERIES, QUERIES * SLOTS * 5 // 8, SLOTS, 1).astype(jnp.int32)
    stored_grads = normal_values(splits[5], (STORE, GW), GW ** -0.5, 0.125, ((0, 256),))
    return dict(activations=activations, out_grads=out_grads, project_in=project_in, project_out=project_out, lengths=lengths, stored_grads=stored_grads)


def reference(activations, out_grads, project_in, project_out, lengths, stored_grads):
    contract = (((0,), (1,)), ((), ()))
    act_proj = lax.dot_general(project_in, activations, contract, preferred_element_type=jnp.float32)
    grad_proj = lax.dot_general(project_out, out_grads, contract, preferred_element_type=jnp.float32)
    live_mask = jnp.arange(SLOTS, dtype=jnp.int32)[None, :] < lengths[:, None]
    inverse_root = 1.0 / jnp.sqrt(lengths.astype(jnp.float32))
    scale_row = jnp.where(live_mask, inverse_root[:, None], jnp.float32(0.0)).reshape(QUERIES * SLOTS)
    factor_left = act_proj.astype(jnp.bfloat16).reshape(RA, QUERIES, SLOTS)
    factor_right = (grad_proj * scale_row[None, :]).astype(jnp.bfloat16).reshape(RG, QUERIES, SLOTS)
    query_grads = jnp.einsum('iqs,jqs->qij', factor_left.astype(jnp.float32), factor_right.astype(jnp.float32), precision=lax.Precision.HIGHEST)
    query_grads = query_grads.reshape(QUERIES, RA * RG).astype(jnp.bfloat16)
    blocks = stored_grads.reshape(STORE // STORE_DEV, STORE_DEV, RA * RG)

    def block_scores(block_rows):
        return lax.dot_general(query_grads, block_rows, (((1,), (1,)), ((), ())), preferred_element_type=jnp.float32).astype(jnp.bfloat16)
    scores = lax.map(block_scores, blocks)
    return jnp.transpose(scores, (1, 0, 2)).reshape(QUERIES, STORE)
```

```python
import functools

import jax
import jax.numpy as jnp
from jax import lax
from jax.experimental import pallas as pl
from jax.experimental.pallas import tpu as pltpu
from jax.sharding import Mesh
from jax.sharding import PartitionSpec as P

F32 = jnp.float32
BF16 = jnp.bfloat16
NT = (((1,), (1,)), ((), ()))
PLANE = ("y", "x")
LINE = ("zh", "zl")


def project_kernel(win_ref, wout_ref, act_ref, grad_ref, out_ref):
    parts = out_ref.shape[0]
    width = win_ref.shape[0]
    for b in range(parts):
        rows = pl.ds(b * 128, 128)
        left = lax.dot_general(win_ref[...], act_ref[rows, :], NT, preferred_element_type=F32)
        right = lax.dot_general(wout_ref[...], grad_ref[rows, :], NT, preferred_element_type=F32)
        out_ref[b, :width, :] = left.astype(BF16)
        out_ref[b, width:, :] = right.astype(BF16)


def project(win, wout, activations, out_grads):
    tokens, feats = activations.shape
    total = win.shape[0] + wout.shape[0]
    steps = 4
    block = tokens // steps
    return pl.pallas_call(
        project_kernel,
        grid=(steps,),
        out_shape=jax.ShapeDtypeStruct((tokens // 128, total, 128), BF16),
        in_specs=[
            pl.BlockSpec(win.shape, lambda i: (0, 0)),
            pl.BlockSpec(wout.shape, lambda i: (0, 0)),
            pl.BlockSpec((block, feats), lambda i: (i, 0)),
            pl.BlockSpec((block, feats), lambda i: (i, 0)),
        ],
        out_specs=pl.BlockSpec((block // 128, total, 128), lambda i: (i, 0, 0)),
        cost_estimate=pl.CostEstimate(
            flops=2 * tokens * feats * total, bytes_accessed=4 * tokens * feats, transcendentals=0
        ),
        name="project",
    )(win, wout, activations, out_grads)


def scale_kernel(slots, width, start_ref, lengths_ref, parts_ref, out_ref):
    tokens = parts_ref.shape[2]
    per = tokens // slots
    lane = lax.broadcasted_iota(jnp.int32, (1, tokens), 1)
    count = jnp.full((1, tokens), 1, jnp.int32)
    for k in range(per):
        count = jnp.where(lane // slots == k, lengths_ref[start_ref[0] + k], count)
    scale = jnp.where(lane % slots < count, 1.0 / jnp.sqrt(count.astype(F32)), 0.0)
    total = jnp.sum(parts_ref[...].astype(F32), axis=0)
    left = total[:width].astype(BF16)
    right = (total[width:] * scale).astype(BF16)
    for d in range(out_ref.shape[0]):
        out_ref[d, :width, :] = left
        out_ref[d, width:, :] = right


def scaled_sum(start, lengths, parts, copies, slots, width):
    smem = pl.BlockSpec(memory_space=pltpu.SMEM)
    vmem = pl.BlockSpec(memory_space=pltpu.VMEM)
    return pl.pallas_call(
        functools.partial(scale_kernel, slots, width),
        out_shape=jax.ShapeDtypeStruct((copies,) + parts.shape[1:], BF16),
        in_specs=[smem, smem, vmem],
        out_specs=vmem,
        name="scaled_sum",
    )(start, lengths, parts)


def outer_kernel(slots, width, parts_ref, out_ref, scratch):
    both, total, tokens = parts_ref.shape
    lines = both // 2
    per = tokens // slots
    other = total - width
    lane = lax.broadcasted_iota(jnp.int32, (width, tokens), 1)
    for z in range(lines):
        summed = (parts_ref[z].astype(F32) + parts_ref[lines + z].astype(F32)).astype(BF16)
        left = summed[:width]
        zero = jnp.zeros_like(left)
        masked = jnp.concatenate(
            [jnp.where(lane // slots == k, left, zero) for k in range(per)], axis=0
        )
        outer = lax.dot_general(masked, summed[width:], NT, preferred_element_type=F32)
        scratch[pl.ds(z * per * width, per * width), :other] = outer
    queries = lines * per
    for m in range(width // 2):
        even = scratch[pl.ds(2 * m, queries, stride=width), :other]
        odd = scratch[pl.ds(2 * m + 1, queries, stride=width), :other]
        pair = jnp.concatenate([even, odd], axis=1).astype(BF16)
        for d in range(out_ref.shape[0]):
            out_ref[d, :, m * 128 : (m + 1) * 128] = pair


def outer_products(parts, copies, slots, width):
    both, total, tokens = parts.shape
    queries = both // 2 * (tokens // slots)
    vmem = pl.BlockSpec(memory_space=pltpu.VMEM)
    return pl.pallas_call(
        functools.partial(outer_kernel, slots, width),
        out_shape=jax.ShapeDtypeStruct((copies, queries, width * (total - width)), BF16),
        in_specs=[vmem],
        out_specs=vmem,
        scratch_shapes=[pltpu.VMEM((queries * width, 128), F32)],
        name="outer_products",
    )(parts)


def score_kernel(side_ref, query_ref, stored_ref, *rest):
    out_ref = rest[-1]
    del side_ref
    plane, queries, depth = query_ref.shape
    acc = lax.dot_general(
        query_ref[...].reshape(plane * queries, depth),
        stored_ref[...],
        NT,
        preferred_element_type=F32,
    )
    columns = acc.shape[1]
    tiles = acc.reshape(plane // 2, 2, queries // 8, 8, columns)
    low = lax.broadcasted_iota(jnp.int32, (8, columns), 0) < 4
    for pair in range(queries // 8):
        for p in range(0, plane // 2, 2):
            firsts, seconds = [], []
            for u in (p, p + 1):
                a, b = tiles[u, 0, pair], tiles[u, 1, pair]
                firsts.append(jnp.where(low, a, pltpu.roll(b, 4, 0)))
                seconds.append(jnp.where(low, pltpu.roll(a, 4, 0), b))
            rows = pl.ds(p * 8, 16)
            out_ref[2 * pair, 0, rows, :] = jnp.concatenate(firsts, axis=0).astype(BF16)
            out_ref[2 * pair + 1, 0, rows, :] = jnp.concatenate(seconds, axis=0).astype(BF16)


def half_scores(side, gathered, stored, previous, lines):
    plane, queries, depth = gathered.shape
    store = stored.shape[0]
    block = 256
    per = queries // lines
    in_specs = [
        pl.BlockSpec((plane, queries, depth), lambda j, s: (0, 0, 0)),
        pl.BlockSpec((block, depth), lambda j, s: (j, 0)),
    ]
    args = [side, gathered, stored]
    aliases = {}
    if previous is not None:
        in_specs.append(pl.BlockSpec(memory_space=pl.ANY))
        args.append(previous)
        aliases = {3: 0}
    return pl.pallas_call(
        score_kernel,
        out_shape=jax.ShapeDtypeStruct((lines, 2, plane * per, store), BF16),
        grid_spec=pltpu.PrefetchScalarGridSpec(
            num_scalar_prefetch=1,
            grid=(store // block,),
            in_specs=in_specs,
            out_specs=pl.BlockSpec((lines, 1, plane * per, block), lambda j, s: (0, s[0], 0, j)),
        ),
        input_output_aliases=aliases,
        cost_estimate=pl.CostEstimate(
            flops=2 * plane * queries * depth * store,
            bytes_accessed=2 * store * depth,
            transcendentals=0,
        ),
        name="half_scores",
    )(*args)


def per_device(activations, out_grads, project_in, project_out, lengths, stored_grads):
    slots = activations.shape[0] // lengths.shape[0]
    width = project_in.shape[1]
    plane = lax.axis_size(PLANE)
    lines = lax.axis_size("zl")
    place = lax.axis_index(PLANE)
    core = lax.axis_index("c")
    per = lengths.shape[0] // plane

    def exchange(values, axes):
        return lax.all_to_all(values, axes, 0, 0, tiled=True)

    partial = project(project_in.T, project_out.T, activations, out_grads)
    partial = exchange(partial, PLANE)
    start = (place * per).astype(jnp.int32).reshape(1)
    halves = scaled_sum(start, lengths, partial, 2 * lines, slots, width)
    halves = exchange(halves, LINE)
    queries = outer_products(halves, plane, slots, width)
    gathered = exchange(queries, PLANE)
    swapped = lax.ppermute(gathered, "c", [(0, 1), (1, 0)])
    side = core.astype(jnp.int32).reshape(1)
    scores = half_scores(side, gathered, stored_grads, None, lines)
    scores = half_scores(1 - side, swapped, stored_grads, scores, lines)
    return scores.reshape(-1, stored_grads.shape[0])


def solution(mesh):
    fine = Mesh(mesh.devices.reshape(4, 4, 2, 4, 2), ("y", "x", "zh", "zl", "c"))
    feat, lane = ("y", "x", "zh"), ("zl", "c")
    placed = (
        P(lane, feat),
        P(lane, feat),
        P(feat, None),
        P(feat, None),
        P(lane),
        P(feat + lane, None),
    )
    return jax.shard_map(
        per_device, mesh=fine, in_specs=placed, out_specs=P(None, feat + lane), check_vma=False
    )
```

```python
import functools

import jax
import jax.numpy as jnp
from jax import lax
from jax.experimental import pallas as pl
from jax.experimental.pallas import tpu as pltpu
from jax.sharding import Mesh
from jax.sharding import PartitionSpec as P

F32 = jnp.float32
BF16 = jnp.bfloat16
NT = (((1,), (1,)), ((), ()))
PLANE = ("y", "x")
LINE = ("zh", "zl")


def project_kernel(
    slots,
    lengths_hbm,
    win_hbm,
    wout_hbm,
    act_hbm,
    grad_hbm,
    out_ref,
    scale_ref,
    lengths,
    win,
    wout,
    act,
    grad,
    sems,
    chunk_sems,
):
    steps, block = chunk_sems.shape[1], act.shape[0] // chunk_sems.shape[1]
    width = win.shape[0]
    small = [
        pltpu.make_async_copy(win_hbm, win, sems.at[0]),
        pltpu.make_async_copy(wout_hbm, wout, sems.at[1]),
        pltpu.make_async_copy(lengths_hbm, lengths, sems.at[2]),
    ]
    for copy in small:
        copy.start()
    chunks = []
    for b in range(steps):
        rows = pl.ds(b * block, block)
        pair = [
            pltpu.make_async_copy(act_hbm.at[rows], act.at[rows], chunk_sems.at[0, b]),
            pltpu.make_async_copy(grad_hbm.at[rows], grad.at[rows], chunk_sems.at[1, b]),
        ]
        for copy in pair:
            copy.start()
        chunks.append(pair)
    for copy in small:
        copy.wait()
    per = 128 // slots
    start = (lax.axis_index("y") * lax.axis_size("x") + lax.axis_index("x")) * per
    lane = lax.broadcasted_iota(jnp.int32, scale_ref.shape, 1)
    count = jnp.full(scale_ref.shape, 1, jnp.int32)
    for k in range(per):
        count = jnp.where(lane // slots == k, lengths[start + k], count)
    scale_ref[...] = jnp.where(lane % slots < count, 1.0 / jnp.sqrt(count.astype(F32)), 0.0)
    for b in range(steps):
        rows = pl.ds(b * block, block)
        chunks[b][0].wait()
        chunks[b][1].wait()
        left = lax.dot_general(win[...], act[rows, :], NT, preferred_element_type=F32)
        right = lax.dot_general(wout[...], grad[rows, :], NT, preferred_element_type=F32)
        for t in range(block // 128):
            at = b * (block // 128) + t
            cols = slice(t * 128, (t + 1) * 128)
            out_ref[at, :width, :] = left[:, cols].astype(BF16)
            out_ref[at, width:, :] = right[:, cols].astype(BF16)


def project(lengths, win, wout, activations, out_grads, slots):
    tokens, feats = activations.shape
    total = win.shape[0] + wout.shape[0]
    steps = 2
    operands = (lengths, win, wout, activations, out_grads)
    hbm = pl.BlockSpec(memory_space=pltpu.HBM)
    vmem = pl.BlockSpec(memory_space=pltpu.VMEM)
    return pl.pallas_call(
        functools.partial(project_kernel, slots),
        out_shape=[
            jax.ShapeDtypeStruct((tokens // 128, total, 128), BF16),
            jax.ShapeDtypeStruct((8, 128), F32),
        ],
        in_specs=[hbm] * len(operands),
        out_specs=[vmem, vmem],
        scratch_shapes=[
            pltpu.SMEM(lengths.shape, jnp.int32),
            pltpu.VMEM(win.shape, BF16),
            pltpu.VMEM(wout.shape, BF16),
            pltpu.VMEM(activations.shape, BF16),
            pltpu.VMEM(out_grads.shape, BF16),
            pltpu.SemaphoreType.DMA((3,)),
            pltpu.SemaphoreType.DMA((2, steps)),
        ],
        compiler_params=pltpu.CompilerParams(vmem_limit_bytes=10 << 20),
        cost_estimate=pl.CostEstimate(
            flops=2 * tokens * feats * total, bytes_accessed=4 * tokens * feats, transcendentals=0
        ),
        name="project",
    )(*[pltpu.with_memory_space_constraint(v, pltpu.HBM) for v in operands])


def scale_kernel(width, parts_ref, scale_ref, out_ref):
    total = jnp.sum(parts_ref[...].astype(F32), axis=0)
    left = total[:width].astype(BF16)
    right = (total[width:] * scale_ref[0:1, :]).astype(BF16)
    for d in range(out_ref.shape[0]):
        out_ref[d, :width, :] = left
        out_ref[d, width:, :] = right


def scaled_sum(parts, scale, copies, width):
    vmem = pl.BlockSpec(memory_space=pltpu.VMEM)
    return pl.pallas_call(
        functools.partial(scale_kernel, width),
        out_shape=jax.ShapeDtypeStruct((copies,) + parts.shape[1:], BF16),
        in_specs=[vmem, vmem],
        out_specs=vmem,
        compiler_params=pltpu.CompilerParams(vmem_limit_bytes=4 << 20),
        cost_estimate=pl.CostEstimate(flops=1000000000, bytes_accessed=1 << 20, transcendentals=0),
        name="scaled_sum",
    )(parts, scale)


def outer_kernel(slots, width, parts_ref, out_ref, scratch):
    both, total, tokens = parts_ref.shape
    lines = both // 2
    per = tokens // slots
    other = total - width
    lane = lax.broadcasted_iota(jnp.int32, (width, tokens), 1)
    for z in range(lines):
        summed = (parts_ref[z].astype(F32) + parts_ref[lines + z].astype(F32)).astype(BF16)
        left = summed[:width]
        zero = jnp.zeros_like(left)
        masked = jnp.concatenate(
            [jnp.where(lane // slots == k, left, zero) for k in range(per)], axis=0
        )
        outer = lax.dot_general(masked, summed[width:], NT, preferred_element_type=F32)
        scratch[pl.ds(z * per * width, per * width), :other] = outer
    queries = lines * per
    for m in range(width // 2):
        even = scratch[pl.ds(2 * m, queries, stride=width), :other]
        odd = scratch[pl.ds(2 * m + 1, queries, stride=width), :other]
        pair = jnp.concatenate([even, odd], axis=1).astype(BF16)
        for d in range(out_ref.shape[0]):
            out_ref[d, :, m * 128 : (m + 1) * 128] = pair


def outer_products(parts, copies, slots, width):
    both, total, tokens = parts.shape
    queries = both // 2 * (tokens // slots)
    vmem = pl.BlockSpec(memory_space=pltpu.VMEM)
    return pl.pallas_call(
        functools.partial(outer_kernel, slots, width),
        out_shape=jax.ShapeDtypeStruct((copies, queries, width * (total - width)), BF16),
        in_specs=[vmem],
        out_specs=vmem,
        scratch_shapes=[pltpu.VMEM((queries * width, 128), F32)],
        compiler_params=pltpu.CompilerParams(vmem_limit_bytes=6 << 20),
        name="outer_products",
    )(parts)


def place_rows(acc, out_ref, plane, queries, cols):
    columns = acc.shape[1]
    tiles = acc.reshape(plane // 2, 2, queries // 8, 8, columns)
    low = lax.broadcasted_iota(jnp.int32, (8, columns), 0) < 4
    for pair in range(queries // 8):
        for p in range(0, plane // 2, 2):
            firsts, seconds = [], []
            for u in (p, p + 1):
                a, b = tiles[u, 0, pair], tiles[u, 1, pair]
                firsts.append(jnp.where(low, a, pltpu.roll(b, 4, 0)))
                seconds.append(jnp.where(low, pltpu.roll(a, 4, 0), b))
            rows = pl.ds(p * 8, 16)
            out_ref[2 * pair, rows, cols] = jnp.concatenate(firsts, axis=0).astype(BF16)
            out_ref[2 * pair + 1, rows, cols] = jnp.concatenate(seconds, axis=0).astype(BF16)


def score_chunks(side, query_ref, stored, out_hbm, staged, sems):
    steps = sems.shape[0]
    block = stored.shape[0] // steps
    plane, queries, depth = query_ref.shape
    sends = []
    for b in range(steps):
        cols = pl.ds(b * block, block)
        acc = lax.dot_general(
            query_ref[...].reshape(plane * queries, depth),
            stored[cols, :],
            NT,
            preferred_element_type=F32,
        )
        place_rows(acc, staged, plane, queries, cols)
        send = pltpu.make_async_copy(
            staged.at[:, :, cols], out_hbm.at[:, side, :, cols], sems.at[b]
        )
        send.start()
        sends.append(send)
    for send in sends:
        send.wait()


def own_kernel(query_ref, kept_ref, out_hbm, staged, sems):
    side = lax.axis_index("c")
    score_chunks(side, query_ref, kept_ref, out_hbm, staged, sems)


def other_kernel(query_ref, kept_ref, previous, out_hbm, staged, sems):
    del previous
    side = 1 - lax.axis_index("c")
    score_chunks(side, query_ref, kept_ref, out_hbm, staged, sems)


def scores_of(gathered, swapped, stored, lines):
    plane, queries, depth = gathered.shape
    store = stored.shape[0]
    rows = plane * queries // lines
    shape = jax.ShapeDtypeStruct((lines, 2, rows, store), BF16)
    hbm = pl.BlockSpec(memory_space=pltpu.HBM)
    vmem = pl.BlockSpec(memory_space=pltpu.VMEM)
    cost = pl.CostEstimate(
        flops=2 * plane * queries * depth * store,
        bytes_accessed=2 * store * depth,
        transcendentals=0,
    )
    params = pltpu.CompilerParams(vmem_limit_bytes=12 << 20)
    scores = pl.pallas_call(
        own_kernel,
        out_shape=shape,
        in_specs=[vmem, vmem],
        out_specs=hbm,
        scratch_shapes=[
            pltpu.VMEM((lines, rows, store), BF16),
            pltpu.SemaphoreType.DMA((1,)),
        ],
        compiler_params=params,
        cost_estimate=cost,
        name="own_half",
    )(gathered, stored)
    return pl.pallas_call(
        other_kernel,
        out_shape=shape,
        in_specs=[vmem, vmem, hbm],
        out_specs=hbm,
        scratch_shapes=[
            pltpu.VMEM((lines, rows, store), BF16),
            pltpu.SemaphoreType.DMA((1,)),
        ],
        input_output_aliases={2: 0},
        compiler_params=params,
        cost_estimate=cost,
        name="other_half",
    )(swapped, stored, scores)


def per_device(activations, out_grads, project_in, project_out, lengths, stored_grads):
    slots = activations.shape[0] // lengths.shape[0]
    width = project_in.shape[1]
    plane = lax.axis_size(PLANE)
    lines = lax.axis_size("zl")

    def exchange(values, axes):
        return lax.all_to_all(values, axes, 0, 0, tiled=True)

    partial, scale = project(
        lengths, project_in.T, project_out.T, activations, out_grads, slots
    )
    partial = exchange(partial, PLANE)
    halves = scaled_sum(partial, scale, 2 * lines, width)
    halves = exchange(halves, LINE)
    queries = outer_products(halves, plane, slots, width)
    gathered = exchange(queries, PLANE)
    swapped = lax.ppermute(gathered, "c", [(0, 1), (1, 0)])
    scores = scores_of(gathered, swapped, stored_grads, lines)
    return scores.reshape(-1, stored_grads.shape[0])


def solution(mesh):
    fine = Mesh(mesh.devices.reshape(4, 4, 2, 4, 2), ("y", "x", "zh", "zl", "c"))
    feat, lane = ("y", "x", "zh"), ("zl", "c")
    placed = (
        P(lane, feat),
        P(lane, feat),
        P(feat, None),
        P(feat, None),
        P(lane),
        P(feat + lane, None),
    )
    return jax.shard_map(
        per_device, mesh=fine, in_specs=placed, out_specs=P(None, feat + lane), check_vma=False
    )
```

```python
import functools

import jax
import jax.numpy as jnp
from jax import lax
from jax.experimental import pallas as pl
from jax.experimental.pallas import tpu as pltpu
from jax.sharding import Mesh
from jax.sharding import PartitionSpec as P

F32 = jnp.float32
BF16 = jnp.bfloat16
NT = (((1,), (1,)), ((), ()))
PLANE = ("y", "x")
LINE = ("zh", "zl")


def project_kernel(
    slots,
    lengths_hbm,
    win_hbm,
    wout_hbm,
    act_hbm,
    grad_hbm,
    out_ref,
    scale_ref,
    lengths,
    win,
    wout,
    act,
    grad,
    sems,
    chunk_sems,
):
    steps, block = chunk_sems.shape[1], act.shape[0] // chunk_sems.shape[1]
    width = win.shape[0]
    small = [
        pltpu.make_async_copy(win_hbm, win, sems.at[0]),
        pltpu.make_async_copy(wout_hbm, wout, sems.at[1]),
        pltpu.make_async_copy(lengths_hbm, lengths, sems.at[2]),
    ]
    chunks = []
    for b in range(steps):
        rows = pl.ds(b * block, block)
        pair = [
            pltpu.make_async_copy(act_hbm.at[rows], act.at[rows], chunk_sems.at[0, b]),
            pltpu.make_async_copy(grad_hbm.at[rows], grad.at[rows], chunk_sems.at[1, b]),
        ]
        for copy in pair + (small if b == 0 else []):
            copy.start()
        chunks.append(pair)
    for copy in small:
        copy.wait()
    per = 128 // slots
    start = (lax.axis_index("y") * lax.axis_size("x") + lax.axis_index("x")) * per
    lane = lax.broadcasted_iota(jnp.int32, scale_ref.shape, 1)
    count = jnp.full(scale_ref.shape, 1, jnp.int32)
    for k in range(per):
        count = jnp.where(lane // slots == k, lengths[start + k], count)
    scale_ref[...] = jnp.where(lane % slots < count, 1.0 / jnp.sqrt(count.astype(F32)), 0.0)
    for b in range(steps):
        rows = pl.ds(b * block, block)
        chunks[b][0].wait()
        chunks[b][1].wait()
        left = lax.dot_general(win[...], act[rows, :], NT, preferred_element_type=F32)
        right = lax.dot_general(wout[...], grad[rows, :], NT, preferred_element_type=F32)
        for t in range(block // 128):
            at = b * (block // 128) + t
            cols = slice(t * 128, (t + 1) * 128)
            out_ref[at, :width, :] = left[:, cols].astype(BF16)
            out_ref[at, width:, :] = right[:, cols].astype(BF16)


def project(lengths, win, wout, activations, out_grads, slots):
    tokens, feats = activations.shape
    total = win.shape[0] + wout.shape[0]
    steps = 2
    operands = (lengths, win, wout, activations, out_grads)
    hbm = pl.BlockSpec(memory_space=pltpu.HBM)
    vmem = pl.BlockSpec(memory_space=pltpu.VMEM)
    return pl.pallas_call(
        functools.partial(project_kernel, slots),
        out_shape=[
            jax.ShapeDtypeStruct((tokens // 128, total, 128), BF16),
            jax.ShapeDtypeStruct((8, 128), F32),
        ],
        in_specs=[hbm] * len(operands),
        out_specs=[vmem, vmem],
        scratch_shapes=[
            pltpu.SMEM(lengths.shape, jnp.int32),
            pltpu.VMEM(win.shape, BF16),
            pltpu.VMEM(wout.shape, BF16),
            pltpu.VMEM(activations.shape, BF16),
            pltpu.VMEM(out_grads.shape, BF16),
            pltpu.SemaphoreType.DMA((3,)),
            pltpu.SemaphoreType.DMA((2, steps)),
        ],
        compiler_params=pltpu.CompilerParams(vmem_limit_bytes=10 << 20),
        cost_estimate=pl.CostEstimate(
            flops=2 * tokens * feats * total, bytes_accessed=4 * tokens * feats, transcendentals=0
        ),
        name="project",
    )(*[pltpu.with_memory_space_constraint(v, pltpu.HBM) for v in operands])


def scale_kernel(width, parts_ref, scale_ref, out_ref):
    total = jnp.sum(parts_ref[...].astype(F32), axis=0)
    left = total[:width].astype(BF16)
    right = (total[width:] * scale_ref[0:1, :]).astype(BF16)
    for d in range(out_ref.shape[0]):
        out_ref[d, :width, :] = left
        out_ref[d, width:, :] = right


def scaled_sum(parts, scale, copies, width):
    vmem = pl.BlockSpec(memory_space=pltpu.VMEM)
    return pl.pallas_call(
        functools.partial(scale_kernel, width),
        out_shape=jax.ShapeDtypeStruct((copies,) + parts.shape[1:], BF16),
        in_specs=[vmem, vmem],
        out_specs=vmem,
        compiler_params=pltpu.CompilerParams(vmem_limit_bytes=4 << 20),
        cost_estimate=pl.CostEstimate(flops=1000000000, bytes_accessed=1 << 20, transcendentals=0),
        name="scaled_sum",
    )(parts, scale)


def outer_kernel(slots, width, parts_ref, out_ref, scratch):
    both, total, tokens = parts_ref.shape
    lines = both // 2
    per = tokens // slots
    other = total - width
    lane = lax.broadcasted_iota(jnp.int32, (width, tokens), 1)
    for z in range(lines):
        summed = (parts_ref[z].astype(F32) + parts_ref[lines + z].astype(F32)).astype(BF16)
        left = summed[:width]
        zero = jnp.zeros_like(left)
        masked = jnp.concatenate(
            [jnp.where(lane // slots == k, left, zero) for k in range(per)], axis=0
        )
        outer = lax.dot_general(masked, summed[width:], NT, preferred_element_type=F32)
        scratch[pl.ds(z * per * width, per * width), :other] = outer
    queries = lines * per
    for m in range(width // 2):
        even = scratch[pl.ds(2 * m, queries, stride=width), :other]
        odd = scratch[pl.ds(2 * m + 1, queries, stride=width), :other]
        pair = jnp.concatenate([even, odd], axis=1).astype(BF16)
        for d in range(out_ref.shape[0]):
            out_ref[d, :, m * 128 : (m + 1) * 128] = pair


def outer_products(parts, copies, slots, width):
    both, total, tokens = parts.shape
    queries = both // 2 * (tokens // slots)
    vmem = pl.BlockSpec(memory_space=pltpu.VMEM)
    return pl.pallas_call(
        functools.partial(outer_kernel, slots, width),
        out_shape=jax.ShapeDtypeStruct((copies, queries, width * (total - width)), BF16),
        in_specs=[vmem],
        out_specs=vmem,
        scratch_shapes=[pltpu.VMEM((queries * width, 128), F32)],
        compiler_params=pltpu.CompilerParams(vmem_limit_bytes=6 << 20),
        name="outer_products",
    )(parts)


def place_rows(acc, out_ref, plane, queries):
    columns = acc.shape[1]
    tiles = acc.reshape(plane // 2, 2, queries // 8, 8, columns)
    low = lax.broadcasted_iota(jnp.int32, (8, columns), 0) < 4
    for pair in range(queries // 8):
        for p in range(0, plane // 2, 2):
            firsts, seconds = [], []
            for u in (p, p + 1):
                a, b = tiles[u, 0, pair], tiles[u, 1, pair]
                firsts.append(jnp.where(low, a, pltpu.roll(b, 4, 0)))
                seconds.append(jnp.where(low, pltpu.roll(a, 4, 0), b))
            rows = pl.ds(p * 8, 16)
            out_ref[2 * pair, rows, :] = jnp.concatenate(firsts, axis=0).astype(BF16)
            out_ref[2 * pair + 1, rows, :] = jnp.concatenate(seconds, axis=0).astype(BF16)


def half_scores(query_ref, stored_ref, out_ref):
    plane, queries, depth = query_ref.shape
    acc = lax.dot_general(
        query_ref[...].reshape(plane * queries, depth),
        stored_ref[...],
        NT,
        preferred_element_type=F32,
    )
    place_rows(acc, out_ref, plane, queries)


def own_kernel(query_ref, stored_ref, out_ref):
    half_scores(query_ref, stored_ref, out_ref)


def other_kernel(query_ref, stored_ref, own_ref, out_hbm, staged, sems):
    side = lax.axis_index("c")
    first = pltpu.make_async_copy(own_ref, out_hbm.at[:, side], sems.at[0])
    first.start()
    half_scores(query_ref, stored_ref, staged)
    second = pltpu.make_async_copy(staged, out_hbm.at[:, 1 - side], sems.at[1])
    second.start()
    first.wait()
    second.wait()


def scores_of(gathered, swapped, stored, lines):
    plane, queries, depth = gathered.shape
    store = stored.shape[0]
    rows = plane * queries // lines
    vmem = pl.BlockSpec(memory_space=pltpu.VMEM)
    cost = pl.CostEstimate(
        flops=2 * plane * queries * depth * store,
        bytes_accessed=2 * store * depth,
        transcendentals=0,
    )
    own = pl.pallas_call(
        own_kernel,
        out_shape=jax.ShapeDtypeStruct((lines, rows, store), BF16),
        in_specs=[vmem, vmem],
        out_specs=vmem,
        compiler_params=pltpu.CompilerParams(vmem_limit_bytes=12 << 20),
        cost_estimate=cost,
        name="own_half",
    )(gathered, stored)
    return pl.pallas_call(
        other_kernel,
        out_shape=jax.ShapeDtypeStruct((lines, 2, rows, store), BF16),
        in_specs=[vmem, vmem, vmem],
        out_specs=pl.BlockSpec(memory_space=pltpu.HBM),
        scratch_shapes=[
            pltpu.VMEM((lines, rows, store), BF16),
            pltpu.SemaphoreType.DMA((2,)),
        ],
        compiler_params=pltpu.CompilerParams(vmem_limit_bytes=12 << 20),
        cost_estimate=cost,
        name="other_half",
    )(swapped, stored, own)


def per_device(activations, out_grads, project_in, project_out, lengths, stored_grads):
    slots = activations.shape[0] // lengths.shape[0]
    width = project_in.shape[1]
    plane = lax.axis_size(PLANE)
    lines = lax.axis_size("zl")

    def exchange(values, axes):
        return lax.all_to_all(values, axes, 0, 0, tiled=True)

    partial, scale = project(
        lengths, project_in.T, project_out.T, activations, out_grads, slots
    )
    partial = exchange(partial, PLANE)
    halves = scaled_sum(partial, scale, 2 * lines, width)
    halves = exchange(halves, LINE)
    queries = outer_products(halves, plane, slots, width)
    gathered = exchange(queries, PLANE)
    swapped = lax.ppermute(gathered, "c", [(0, 1), (1, 0)])
    scores = scores_of(gathered, swapped, stored_grads, lines)
    return scores.reshape(-1, stored_grads.shape[0])


def solution(mesh):
    fine = Mesh(mesh.devices.reshape(4, 4, 2, 4, 2), ("y", "x", "zh", "zl", "c"))
    feat, lane = ("y", "x", "zh"), ("zl", "c")
    placed = (
        P(lane, feat),
        P(lane, feat),
        P(feat, None),
        P(feat, None),
        P(lane),
        P(feat + lane, None),
    )
    return jax.shard_map(
        per_device, mesh=fine, in_specs=placed, out_specs=P(None, feat + lane), check_vma=False
    )
```

```python
import functools

import jax
import jax.numpy as jnp
from jax import lax
from jax.experimental import pallas as pl
from jax.experimental.pallas import tpu as pltpu
from jax.sharding import Mesh
from jax.sharding import PartitionSpec as P

F32 = jnp.float32
BF16 = jnp.bfloat16
NT = (((1,), (1,)), ((), ()))
PLANE = ("y", "x")
LINE = ("zh", "zl")


def project_kernel(
    slots,
    lengths_hbm,
    win_hbm,
    wout_hbm,
    act_hbm,
    grad_hbm,
    out_ref,
    scale_ref,
    lengths,
    win,
    wout,
    act,
    grad,
    sems,
    chunk_sems,
):
    steps, block = chunk_sems.shape[1], act.shape[0] // chunk_sems.shape[1]
    width = win.shape[0]
    small = [
        pltpu.make_async_copy(win_hbm, win, sems.at[0]),
        pltpu.make_async_copy(wout_hbm, wout, sems.at[1]),
        pltpu.make_async_copy(lengths_hbm, lengths, sems.at[2]),
    ]
    chunks = []
    for b in range(steps):
        rows = pl.ds(b * block, block)
        pair = [
            pltpu.make_async_copy(act_hbm.at[rows], act.at[rows], chunk_sems.at[0, b]),
            pltpu.make_async_copy(grad_hbm.at[rows], grad.at[rows], chunk_sems.at[1, b]),
        ]
        for copy in pair + (small if b == 0 else []):
            copy.start()
        chunks.append(pair)
    for copy in small:
        copy.wait()
    per = 128 // slots
    start = (lax.axis_index("y") * lax.axis_size("x") + lax.axis_index("x")) * per
    lane = lax.broadcasted_iota(jnp.int32, scale_ref.shape, 1)
    count = jnp.full(scale_ref.shape, 1, jnp.int32)
    for k in range(per):
        count = jnp.where(lane // slots == k, lengths[start + k], count)
    scale_ref[...] = jnp.where(lane % slots < count, 1.0 / jnp.sqrt(count.astype(F32)), 0.0)
    for b in range(steps):
        rows = pl.ds(b * block, block)
        chunks[b][0].wait()
        chunks[b][1].wait()
        left = lax.dot_general(win[...], act[rows, :], NT, preferred_element_type=F32)
        right = lax.dot_general(wout[...], grad[rows, :], NT, preferred_element_type=F32)
        for t in range(block // 128):
            at = b * (block // 128) + t
            cols = slice(t * 128, (t + 1) * 128)
            out_ref[at, :width, :] = left[:, cols].astype(BF16)
            out_ref[at, width:, :] = right[:, cols].astype(BF16)


def project(lengths, win, wout, activations, out_grads, slots):
    tokens, feats = activations.shape
    total = win.shape[0] + wout.shape[0]
    steps = 2
    operands = (lengths, win, wout, activations, out_grads)
    hbm = pl.BlockSpec(memory_space=pltpu.HBM)
    vmem = pl.BlockSpec(memory_space=pltpu.VMEM)
    return pl.pallas_call(
        functools.partial(project_kernel, slots),
        out_shape=[
            jax.ShapeDtypeStruct((tokens // 128, total, 128), BF16),
            jax.ShapeDtypeStruct((8, 128), F32),
        ],
        in_specs=[hbm] * len(operands),
        out_specs=[vmem, vmem],
        scratch_shapes=[
            pltpu.SMEM(lengths.shape, jnp.int32),
            pltpu.VMEM(win.shape, BF16),
            pltpu.VMEM(wout.shape, BF16),
            pltpu.VMEM(activations.shape, BF16),
            pltpu.VMEM(out_grads.shape, BF16),
            pltpu.SemaphoreType.DMA((3,)),
            pltpu.SemaphoreType.DMA((2, steps)),
        ],
        compiler_params=pltpu.CompilerParams(vmem_limit_bytes=10 << 20),
        cost_estimate=pl.CostEstimate(
            flops=2 * tokens * feats * total, bytes_accessed=4 * tokens * feats, transcendentals=0
        ),
        name="project",
    )(*[pltpu.with_memory_space_constraint(v, pltpu.HBM) for v in operands])


def scale_kernel(width, parts_ref, scale_ref, out_ref):
    total = jnp.sum(parts_ref[...].astype(F32), axis=0)
    left = total[:width].astype(BF16)
    right = (total[width:] * scale_ref[0:1, :]).astype(BF16)
    for d in range(out_ref.shape[0]):
        out_ref[d, :width, :] = left
        out_ref[d, width:, :] = right


def scaled_sum(parts, scale, copies, width):
    vmem = pl.BlockSpec(memory_space=pltpu.VMEM)
    return pl.pallas_call(
        functools.partial(scale_kernel, width),
        out_shape=jax.ShapeDtypeStruct((copies,) + parts.shape[1:], BF16),
        in_specs=[vmem, vmem],
        out_specs=vmem,
        compiler_params=pltpu.CompilerParams(vmem_limit_bytes=4 << 20),
        cost_estimate=pl.CostEstimate(flops=1000000000, bytes_accessed=1 << 20, transcendentals=0),
        name="scaled_sum",
    )(parts, scale)


def outer_kernel(slots, width, parts_ref, out_ref, scratch):
    both, total, tokens = parts_ref.shape
    lines = both // 2
    per = tokens // slots
    other = total - width
    lane = lax.broadcasted_iota(jnp.int32, (width, 3 * tokens), 1)
    for z in range(lines):
        summed = parts_ref[z].astype(F32) + parts_ref[lines + z].astype(F32)
        high = summed.astype(BF16)
        low = (summed - high.astype(F32)).astype(BF16)
        left = jnp.concatenate([high[:width], high[:width], low[:width]], axis=1)
        right = jnp.concatenate([high[width:], low[width:], high[width:]], axis=1)
        zero = jnp.zeros_like(left)
        masked = jnp.concatenate(
            [jnp.where(lane % tokens // slots == k, left, zero) for k in range(per)], axis=0
        )
        outer = lax.dot_general(masked, right, NT, preferred_element_type=F32)
        scratch[pl.ds(z * per * width, per * width), :other] = outer
    queries = lines * per
    for m in range(width // 2):
        even = scratch[pl.ds(2 * m, queries, stride=width), :other]
        odd = scratch[pl.ds(2 * m + 1, queries, stride=width), :other]
        pair = jnp.concatenate([even, odd], axis=1).astype(BF16)
        for d in range(out_ref.shape[0]):
            out_ref[d, :, m * 128 : (m + 1) * 128] = pair


def outer_products(parts, copies, slots, width):
    both, total, tokens = parts.shape
    queries = both // 2 * (tokens // slots)
    vmem = pl.BlockSpec(memory_space=pltpu.VMEM)
    return pl.pallas_call(
        functools.partial(outer_kernel, slots, width),
        out_shape=jax.ShapeDtypeStruct((copies, queries, width * (total - width)), BF16),
        in_specs=[vmem],
        out_specs=vmem,
        scratch_shapes=[pltpu.VMEM((queries * width, 128), F32)],
        compiler_params=pltpu.CompilerParams(vmem_limit_bytes=6 << 20),
        name="outer_products",
    )(parts)


def place_rows(acc, out_ref, plane, queries):
    columns = acc.shape[1]
    tiles = acc.reshape(plane // 2, 2, queries // 8, 8, columns)
    low = lax.broadcasted_iota(jnp.int32, (8, columns), 0) < 4
    for pair in range(queries // 8):
        for p in range(0, plane // 2, 2):
            firsts, seconds = [], []
            for u in (p, p + 1):
                a, b = tiles[u, 0, pair], tiles[u, 1, pair]
                firsts.append(jnp.where(low, a, pltpu.roll(b, 4, 0)))
                seconds.append(jnp.where(low, pltpu.roll(a, 4, 0), b))
            rows = pl.ds(p * 8, 16)
            out_ref[2 * pair, rows, :] = jnp.concatenate(firsts, axis=0).astype(BF16)
            out_ref[2 * pair + 1, rows, :] = jnp.concatenate(seconds, axis=0).astype(BF16)


def half_scores(query_ref, stored_ref, out_ref):
    plane, queries, depth = query_ref.shape
    acc = lax.dot_general(
        query_ref[...].reshape(plane * queries, depth),
        stored_ref[...],
        NT,
        preferred_element_type=F32,
    )
    place_rows(acc, out_ref, plane, queries)


def own_kernel(query_ref, stored_ref, out_ref):
    half_scores(query_ref, stored_ref, out_ref)


def other_kernel(query_ref, stored_ref, own_ref, out_hbm, staged, sems):
    side = lax.axis_index("c")
    first = pltpu.make_async_copy(own_ref, out_hbm.at[:, side], sems.at[0])
    first.start()
    half_scores(query_ref, stored_ref, staged)
    second = pltpu.make_async_copy(staged, out_hbm.at[:, 1 - side], sems.at[1])
    second.start()
    first.wait()
    second.wait()


def scores_of(gathered, swapped, stored, lines):
    plane, queries, depth = gathered.shape
    store = stored.shape[0]
    rows = plane * queries // lines
    vmem = pl.BlockSpec(memory_space=pltpu.VMEM)
    cost = pl.CostEstimate(
        flops=2 * plane * queries * depth * store,
        bytes_accessed=2 * store * depth,
        transcendentals=0,
    )
    own = pl.pallas_call(
        own_kernel,
        out_shape=jax.ShapeDtypeStruct((lines, rows, store), BF16),
        in_specs=[vmem, vmem],
        out_specs=vmem,
        compiler_params=pltpu.CompilerParams(vmem_limit_bytes=12 << 20),
        cost_estimate=cost,
        name="own_half",
    )(gathered, stored)
    return pl.pallas_call(
        other_kernel,
        out_shape=jax.ShapeDtypeStruct((lines, 2, rows, store), BF16),
        in_specs=[vmem, vmem, vmem],
        out_specs=pl.BlockSpec(memory_space=pltpu.HBM),
        scratch_shapes=[
            pltpu.VMEM((lines, rows, store), BF16),
            pltpu.SemaphoreType.DMA((2,)),
        ],
        compiler_params=pltpu.CompilerParams(vmem_limit_bytes=12 << 20),
        cost_estimate=cost,
        name="other_half",
    )(swapped, stored, own)


def per_device(activations, out_grads, project_in, project_out, lengths, stored_grads):
    slots = activations.shape[0] // lengths.shape[0]
    width = project_in.shape[1]
    plane = lax.axis_size(PLANE)
    lines = lax.axis_size("zl")

    def exchange(values, axes):
        return lax.all_to_all(values, axes, 0, 0, tiled=True)

    partial, scale = project(
        lengths, project_in.T, project_out.T, activations, out_grads, slots
    )
    partial = exchange(partial, PLANE)
    halves = scaled_sum(partial, scale, 2 * lines, width)
    halves = exchange(halves, LINE)
    queries = outer_products(halves, plane, slots, width)
    gathered = exchange(queries, PLANE)
    swapped = lax.ppermute(gathered, "c", [(0, 1), (1, 0)])
    scores = scores_of(gathered, swapped, stored_grads, lines)
    return scores.reshape(-1, stored_grads.shape[0])


def solution(mesh):
    fine = Mesh(mesh.devices.reshape(4, 4, 2, 4, 2), ("y", "x", "zh", "zl", "c"))
    feat, lane = ("y", "x", "zh"), ("zl", "c")
    placed = (
        P(lane, feat),
        P(lane, feat),
        P(feat, None),
        P(feat, None),
        P(lane),
        P(feat + lane, None),
    )
    return jax.shard_map(
        per_device, mesh=fine, in_specs=placed, out_specs=P(None, feat + lane), check_vma=False
    )
```

```python
import functools

import jax
import jax.numpy as jnp
from jax import lax
from jax.experimental import pallas as pl
from jax.experimental.pallas import tpu as pltpu
from jax.sharding import Mesh
from jax.sharding import PartitionSpec as P

F32 = jnp.float32
BF16 = jnp.bfloat16
NT = (((1,), (1,)), ((), ()))
PLANE = ("x", "y")
LINE = ("zl", "zh")


def project_kernel(
    slots,
    lengths_hbm,
    win_hbm,
    wout_hbm,
    act_hbm,
    grad_hbm,
    out_ref,
    scale_ref,
    lengths,
    win,
    wout,
    act,
    grad,
    sems,
    chunk_sems,
):
    steps, block = chunk_sems.shape[1], act.shape[0] // chunk_sems.shape[1]
    width = win.shape[0]
    small = [
        pltpu.make_async_copy(win_hbm, win, sems.at[0]),
        pltpu.make_async_copy(wout_hbm, wout, sems.at[1]),
        pltpu.make_async_copy(lengths_hbm, lengths, sems.at[2]),
    ]
    chunks = []
    for b in range(steps):
        rows = pl.ds(b * block, block)
        pair = [
            pltpu.make_async_copy(act_hbm.at[rows], act.at[rows], chunk_sems.at[0, b]),
            pltpu.make_async_copy(grad_hbm.at[rows], grad.at[rows], chunk_sems.at[1, b]),
        ]
        for copy in pair + (small if b == 0 else []):
            copy.start()
        chunks.append(pair)
    for copy in small:
        copy.wait()
    per = 128 // slots
    start = (lax.axis_index("x") * lax.axis_size("y") + lax.axis_index("y")) * per
    lane = lax.broadcasted_iota(jnp.int32, scale_ref.shape, 1)
    count = jnp.full(scale_ref.shape, 1, jnp.int32)
    for k in range(per):
        count = jnp.where(lane // slots == k, lengths[start + k], count)
    scale_ref[...] = jnp.where(lane % slots < count, 1.0 / jnp.sqrt(count.astype(F32)), 0.0)
    for b in range(steps):
        rows = pl.ds(b * block, block)
        chunks[b][0].wait()
        chunks[b][1].wait()
        left = lax.dot_general(win[...], act[rows, :], NT, preferred_element_type=F32)
        right = lax.dot_general(wout[...], grad[rows, :], NT, preferred_element_type=F32)
        for t in range(block // 128):
            at = b * (block // 128) + t
            cols = slice(t * 128, (t + 1) * 128)
            out_ref[at, :width, :] = left[:, cols].astype(BF16)
            out_ref[at, width:, :] = right[:, cols].astype(BF16)


def project(lengths, win, wout, activations, out_grads, slots):
    tokens, feats = activations.shape
    total = win.shape[0] + wout.shape[0]
    steps = 2
    operands = (lengths, win, wout, activations, out_grads)
    hbm = pl.BlockSpec(memory_space=pltpu.HBM)
    vmem = pl.BlockSpec(memory_space=pltpu.VMEM)
    return pl.pallas_call(
        functools.partial(project_kernel, slots),
        out_shape=[
            jax.ShapeDtypeStruct((tokens // 128, total, 128), BF16),
            jax.ShapeDtypeStruct((8, 128), F32),
        ],
        in_specs=[hbm] * len(operands),
        out_specs=[vmem, vmem],
        scratch_shapes=[
            pltpu.SMEM(lengths.shape, jnp.int32),
            pltpu.VMEM(win.shape, BF16),
            pltpu.VMEM(wout.shape, BF16),
            pltpu.VMEM(activations.shape, BF16),
            pltpu.VMEM(out_grads.shape, BF16),
            pltpu.SemaphoreType.DMA((3,)),
            pltpu.SemaphoreType.DMA((2, steps)),
        ],
        compiler_params=pltpu.CompilerParams(vmem_limit_bytes=10 << 20),
        cost_estimate=pl.CostEstimate(
            flops=2 * tokens * feats * total, bytes_accessed=4 * tokens * feats, transcendentals=0
        ),
        name="project",
    )(*[pltpu.with_memory_space_constraint(v, pltpu.HBM) for v in operands])


def scale_kernel(width, parts_ref, scale_ref, out_ref):
    total = jnp.sum(parts_ref[...].astype(F32), axis=0)
    left = total[:width].astype(BF16)
    right = (total[width:] * scale_ref[0:1, :]).astype(BF16)
    for d in range(out_ref.shape[0]):
        out_ref[d, :width, :] = left
        out_ref[d, width:, :] = right


def scaled_sum(parts, scale, copies, width):
    vmem = pl.BlockSpec(memory_space=pltpu.VMEM)
    return pl.pallas_call(
        functools.partial(scale_kernel, width),
        out_shape=jax.ShapeDtypeStruct((copies,) + parts.shape[1:], BF16),
        in_specs=[vmem, vmem],
        out_specs=vmem,
        compiler_params=pltpu.CompilerParams(vmem_limit_bytes=4 << 20),
        cost_estimate=pl.CostEstimate(flops=1000000000, bytes_accessed=1 << 20, transcendentals=0),
        name="scaled_sum",
    )(parts, scale)


def outer_kernel(slots, width, parts_ref, out_ref, scratch):
    both, total, tokens = parts_ref.shape
    lines = both // 2
    per = tokens // slots
    other = total - width
    lane = lax.broadcasted_iota(jnp.int32, (width, 3 * tokens), 1)
    for z in range(lines):
        summed = parts_ref[2 * z].astype(F32) + parts_ref[2 * z + 1].astype(F32)
        high = summed.astype(BF16)
        low = (summed - high.astype(F32)).astype(BF16)
        left = jnp.concatenate([high[:width], high[:width], low[:width]], axis=1)
        right = jnp.concatenate([high[width:], low[width:], high[width:]], axis=1)
        zero = jnp.zeros_like(left)
        masked = jnp.concatenate(
            [jnp.where(lane % tokens // slots == k, left, zero) for k in range(per)], axis=0
        )
        outer = lax.dot_general(masked, right, NT, preferred_element_type=F32)
        scratch[pl.ds(z * per * width, per * width), :other] = outer
    queries = lines * per
    for m in range(width // 2):
        even = scratch[pl.ds(2 * m, queries, stride=width), :other]
        odd = scratch[pl.ds(2 * m + 1, queries, stride=width), :other]
        pair = jnp.concatenate([even, odd], axis=1).astype(BF16)
        for d in range(out_ref.shape[0]):
            out_ref[d, :, m * 128 : (m + 1) * 128] = pair


def outer_products(parts, copies, slots, width):
    both, total, tokens = parts.shape
    queries = both // 2 * (tokens // slots)
    vmem = pl.BlockSpec(memory_space=pltpu.VMEM)
    return pl.pallas_call(
        functools.partial(outer_kernel, slots, width),
        out_shape=jax.ShapeDtypeStruct((copies, queries, width * (total - width)), BF16),
        in_specs=[vmem],
        out_specs=vmem,
        scratch_shapes=[pltpu.VMEM((queries * width, 128), F32)],
        compiler_params=pltpu.CompilerParams(vmem_limit_bytes=6 << 20),
        name="outer_products",
    )(parts)


def place_rows(acc, out_ref, plane, queries):
    columns = acc.shape[1]
    tiles = acc.reshape(plane // 2, 2, queries // 8, 8, columns)
    low = lax.broadcasted_iota(jnp.int32, (8, columns), 0) < 4
    for pair in range(queries // 8):
        for p in range(0, plane // 2, 2):
            firsts, seconds = [], []
            for u in (p, p + 1):
                a, b = tiles[u, 0, pair], tiles[u, 1, pair]
                firsts.append(jnp.where(low, a, pltpu.roll(b, 4, 0)))
                seconds.append(jnp.where(low, pltpu.roll(a, 4, 0), b))
            rows = pl.ds(p * 8, 16)
            out_ref[2 * pair, rows, :] = jnp.concatenate(firsts, axis=0).astype(BF16)
            out_ref[2 * pair + 1, rows, :] = jnp.concatenate(seconds, axis=0).astype(BF16)


def half_scores(query_ref, stored_ref, out_ref):
    plane, queries, depth = query_ref.shape
    acc = lax.dot_general(
        query_ref[...].reshape(plane * queries, depth),
        stored_ref[...],
        NT,
        preferred_element_type=F32,
    )
    place_rows(acc, out_ref, plane, queries)


def own_kernel(query_ref, stored_ref, out_ref):
    half_scores(query_ref, stored_ref, out_ref)


def other_kernel(query_ref, stored_ref, own_ref, out_hbm, staged, sems):
    side = lax.axis_index("c")
    lines = staged.shape[0]
    copies = [
        pltpu.make_async_copy(own_ref.at[z], out_hbm.at[z, side], sems.at[0, z])
        for z in range(lines)
    ]
    for copy in copies:
        copy.start()
    half_scores(query_ref, stored_ref, staged)
    for z in range(lines):
        copy = pltpu.make_async_copy(staged.at[z], out_hbm.at[z, 1 - side], sems.at[1, z])
        copy.start()
        copies.append(copy)
    for copy in copies:
        copy.wait()


def scores_of(gathered, swapped, stored, lines):
    plane, queries, depth = gathered.shape
    store = stored.shape[0]
    rows = plane * queries // lines
    vmem = pl.BlockSpec(memory_space=pltpu.VMEM)
    cost = pl.CostEstimate(
        flops=2 * plane * queries * depth * store,
        bytes_accessed=2 * store * depth,
        transcendentals=0,
    )
    own = pl.pallas_call(
        own_kernel,
        out_shape=jax.ShapeDtypeStruct((lines, rows, store), BF16),
        in_specs=[vmem, vmem],
        out_specs=vmem,
        compiler_params=pltpu.CompilerParams(vmem_limit_bytes=12 << 20),
        cost_estimate=cost,
        name="own_half",
    )(gathered, stored)
    return pl.pallas_call(
        other_kernel,
        out_shape=jax.ShapeDtypeStruct((lines, 2, rows, store), BF16),
        in_specs=[vmem, vmem, vmem],
        out_specs=pl.BlockSpec(memory_space=pltpu.HBM),
        scratch_shapes=[
            pltpu.VMEM((lines, rows, store), BF16),
            pltpu.SemaphoreType.DMA((2, lines)),
        ],
        compiler_params=pltpu.CompilerParams(vmem_limit_bytes=12 << 20),
        cost_estimate=cost,
        name="other_half",
    )(swapped, stored, own)


def per_device(activations, out_grads, project_in, project_out, lengths, stored_grads):
    slots = activations.shape[0] // lengths.shape[0]
    width = project_in.shape[1]
    plane = lax.axis_size(PLANE)
    lines = lax.axis_size("zl")

    def exchange(values, axes):
        return lax.all_to_all(values, axes, 0, 0, tiled=True)

    partial, scale = project(
        lengths, project_in.T, project_out.T, activations, out_grads, slots
    )
    partial = exchange(partial, PLANE)
    halves = scaled_sum(partial, scale, 2 * lines, width)
    halves = exchange(halves, LINE)
    queries = outer_products(halves, plane, slots, width)
    gathered = exchange(queries, PLANE)
    swapped = lax.ppermute(gathered, "c", [(0, 1), (1, 0)])
    scores = scores_of(gathered, swapped, stored_grads, lines)
    return scores.reshape(-1, stored_grads.shape[0])


def solution(mesh):
    fine = Mesh(mesh.devices.reshape(4, 4, 2, 4, 2), ("y", "x", "zh", "zl", "c"))
    feat, lane = ("y", "x", "zh"), ("zl", "c")
    placed = (
        P(lane, feat),
        P(lane, feat),
        P(feat, None),
        P(feat, None),
        P(lane),
        P(feat + lane, None),
    )
    return jax.shard_map(
        per_device, mesh=fine, in_specs=placed, out_specs=P(None, feat + lane), check_vma=False
    )
```

```python
import functools

import jax
import jax.numpy as jnp
from jax import lax
from jax.experimental import pallas as pl
from jax.experimental.pallas import tpu as pltpu
from jax.sharding import Mesh
from jax.sharding import PartitionSpec as P

F32 = jnp.float32
BF16 = jnp.bfloat16
NT = (((1,), (1,)), ((), ()))
PLANE = ("y", "x")
LINE = ("zl", "zh")


def project_kernel(
    slots,
    lengths_hbm,
    win_hbm,
    wout_hbm,
    act_hbm,
    grad_hbm,
    out_ref,
    scale_ref,
    lengths,
    win,
    wout,
    act,
    grad,
    sems,
    chunk_sems,
):
    steps, block = chunk_sems.shape[1], act.shape[0] // chunk_sems.shape[1]
    width = win.shape[0]
    small = [
        pltpu.make_async_copy(win_hbm, win, sems.at[0]),
        pltpu.make_async_copy(wout_hbm, wout, sems.at[1]),
        pltpu.make_async_copy(lengths_hbm, lengths, sems.at[2]),
    ]
    chunks = []
    for b in range(steps):
        rows = pl.ds(b * block, block)
        pair = [
            pltpu.make_async_copy(act_hbm.at[rows], act.at[rows], chunk_sems.at[0, b]),
            pltpu.make_async_copy(grad_hbm.at[rows], grad.at[rows], chunk_sems.at[1, b]),
        ]
        for copy in pair + (small if b == 0 else []):
            copy.start()
        chunks.append(pair)
    for copy in small:
        copy.wait()
    per = 128 // slots
    start = (lax.axis_index("y") * lax.axis_size("x") + lax.axis_index("x")) * per
    lane = lax.broadcasted_iota(jnp.int32, scale_ref.shape, 1)
    count = jnp.full(scale_ref.shape, 1, jnp.int32)
    for k in range(per):
        count = jnp.where(lane // slots == k, lengths[start + k], count)
    scale_ref[...] = jnp.where(lane % slots < count, 1.0 / jnp.sqrt(count.astype(F32)), 0.0)
    for b in range(steps):
        rows = pl.ds(b * block, block)
        chunks[b][0].wait()
        chunks[b][1].wait()
        left = lax.dot_general(win[...], act[rows, :], NT, preferred_element_type=F32)
        right = lax.dot_general(wout[...], grad[rows, :], NT, preferred_element_type=F32)
        for t in range(block // 128):
            at = b * (block // 128) + t
            cols = slice(t * 128, (t + 1) * 128)
            out_ref[at, :width, :] = left[:, cols].astype(BF16)
            out_ref[at, width:, :] = right[:, cols].astype(BF16)


def project(lengths, win, wout, activations, out_grads, slots):
    tokens, feats = activations.shape
    total = win.shape[0] + wout.shape[0]
    steps = 2
    operands = (lengths, win, wout, activations, out_grads)
    hbm = pl.BlockSpec(memory_space=pltpu.HBM)
    vmem = pl.BlockSpec(memory_space=pltpu.VMEM)
    return pl.pallas_call(
        functools.partial(project_kernel, slots),
        out_shape=[
            jax.ShapeDtypeStruct((tokens // 128, total, 128), BF16),
            jax.ShapeDtypeStruct((8, 128), F32),
        ],
        in_specs=[hbm] * len(operands),
        out_specs=[vmem, vmem],
        scratch_shapes=[
            pltpu.SMEM(lengths.shape, jnp.int32),
            pltpu.VMEM(win.shape, BF16),
            pltpu.VMEM(wout.shape, BF16),
            pltpu.VMEM(activations.shape, BF16),
            pltpu.VMEM(out_grads.shape, BF16),
            pltpu.SemaphoreType.DMA((3,)),
            pltpu.SemaphoreType.DMA((2, steps)),
        ],
        compiler_params=pltpu.CompilerParams(vmem_limit_bytes=10 << 20),
        cost_estimate=pl.CostEstimate(
            flops=2 * tokens * feats * total, bytes_accessed=4 * tokens * feats, transcendentals=0
        ),
        name="project",
    )(*[pltpu.with_memory_space_constraint(v, pltpu.HBM) for v in operands])


def scale_kernel(width, parts_ref, scale_ref, out_ref):
    total = jnp.sum(parts_ref[...].astype(F32), axis=0)
    left = total[:width].astype(BF16)
    right = (total[width:] * scale_ref[0:1, :]).astype(BF16)
    for d in range(out_ref.shape[0]):
        out_ref[d, :width, :] = left
        out_ref[d, width:, :] = right


def scaled_sum(parts, scale, copies, width):
    vmem = pl.BlockSpec(memory_space=pltpu.VMEM)
    return pl.pallas_call(
        functools.partial(scale_kernel, width),
        out_shape=jax.ShapeDtypeStruct((copies,) + parts.shape[1:], BF16),
        in_specs=[vmem, vmem],
        out_specs=vmem,
        compiler_params=pltpu.CompilerParams(vmem_limit_bytes=4 << 20),
        cost_estimate=pl.CostEstimate(flops=1000000000, bytes_accessed=1 << 20, transcendentals=0),
        name="scaled_sum",
    )(parts, scale)


def outer_kernel(slots, width, parts_ref, out_ref, scratch):
    both, total, tokens = parts_ref.shape
    lines = both // 2
    per = tokens // slots
    other = total - width
    lane = lax.broadcasted_iota(jnp.int32, (width, 3 * tokens), 1)
    for z in range(lines):
        summed = parts_ref[2 * z].astype(F32) + parts_ref[2 * z + 1].astype(F32)
        high = summed.astype(BF16)
        low = (summed - high.astype(F32)).astype(BF16)
        left = jnp.concatenate([high[:width], high[:width], low[:width]], axis=1)
        right = jnp.concatenate([high[width:], low[width:], high[width:]], axis=1)
        zero = jnp.zeros_like(left)
        masked = jnp.concatenate(
            [jnp.where(lane % tokens // slots == k, left, zero) for k in range(per)], axis=0
        )
        outer = lax.dot_general(masked, right, NT, preferred_element_type=F32)
        scratch[pl.ds(z * per * width, per * width), :other] = outer
    queries = lines * per
    for m in range(width // 2):
        even = scratch[pl.ds(2 * m, queries, stride=width), :other]
        odd = scratch[pl.ds(2 * m + 1, queries, stride=width), :other]
        pair = jnp.concatenate([even, odd], axis=1).astype(BF16)
        for d in range(out_ref.shape[0]):
            out_ref[d, :, m * 128 : (m + 1) * 128] = pair


def outer_products(parts, copies, slots, width):
    both, total, tokens = parts.shape
    queries = both // 2 * (tokens // slots)
    vmem = pl.BlockSpec(memory_space=pltpu.VMEM)
    return pl.pallas_call(
        functools.partial(outer_kernel, slots, width),
        out_shape=jax.ShapeDtypeStruct((copies, queries, width * (total - width)), BF16),
        in_specs=[vmem],
        out_specs=vmem,
        scratch_shapes=[pltpu.VMEM((queries * width, 128), F32)],
        compiler_params=pltpu.CompilerParams(vmem_limit_bytes=6 << 20),
        name="outer_products",
    )(parts)


def place_rows(acc, out_ref, plane, queries):
    columns = acc.shape[1]
    tiles = acc.reshape(plane // 2, 2, queries // 8, 8, columns)
    low = lax.broadcasted_iota(jnp.int32, (8, columns), 0) < 4
    for pair in range(queries // 8):
        for p in range(0, plane // 2, 2):
            firsts, seconds = [], []
            for u in (p, p + 1):
                a, b = tiles[u, 0, pair], tiles[u, 1, pair]
                firsts.append(jnp.where(low, a, pltpu.roll(b, 4, 0)))
                seconds.append(jnp.where(low, pltpu.roll(a, 4, 0), b))
            rows = pl.ds(p * 8, 16)
            out_ref[2 * pair, rows, :] = jnp.concatenate(firsts, axis=0).astype(BF16)
            out_ref[2 * pair + 1, rows, :] = jnp.concatenate(seconds, axis=0).astype(BF16)


def half_scores(query_ref, stored_ref, out_ref):
    plane, queries, depth = query_ref.shape
    acc = lax.dot_general(
        query_ref[...].reshape(plane * queries, depth),
        stored_ref[...],
        NT,
        preferred_element_type=F32,
    )
    place_rows(acc, out_ref, plane, queries)


def own_kernel(query_ref, stored_ref, out_ref):
    half_scores(query_ref, stored_ref, out_ref)


def other_kernel(query_ref, stored_ref, own_ref, out_hbm, staged, sems):
    side = lax.axis_index("c")
    lines = staged.shape[0]
    copies = [
        pltpu.make_async_copy(own_ref.at[z], out_hbm.at[z, side], sems.at[0, z])
        for z in range(lines)
    ]
    for copy in copies:
        copy.start()
    half_scores(query_ref, stored_ref, staged)
    for z in range(lines):
        copy = pltpu.make_async_copy(staged.at[z], out_hbm.at[z, 1 - side], sems.at[1, z])
        copy.start()
        copies.append(copy)
    for copy in copies:
        copy.wait()


def scores_of(gathered, swapped, stored, lines):
    plane, queries, depth = gathered.shape
    store = stored.shape[0]
    rows = plane * queries // lines
    vmem = pl.BlockSpec(memory_space=pltpu.VMEM)
    cost = pl.CostEstimate(
        flops=2 * plane * queries * depth * store,
        bytes_accessed=2 * store * depth,
        transcendentals=0,
    )
    own = pl.pallas_call(
        own_kernel,
        out_shape=jax.ShapeDtypeStruct((lines, rows, store), BF16),
        in_specs=[vmem, vmem],
        out_specs=vmem,
        compiler_params=pltpu.CompilerParams(vmem_limit_bytes=12 << 20),
        cost_estimate=cost,
        name="own_half",
    )(gathered, stored)
    return pl.pallas_call(
        other_kernel,
        out_shape=jax.ShapeDtypeStruct((lines, 2, rows, store), BF16),
        in_specs=[vmem, vmem, vmem],
        out_specs=pl.BlockSpec(memory_space=pltpu.HBM),
        scratch_shapes=[
            pltpu.VMEM((lines, rows, store), BF16),
            pltpu.SemaphoreType.DMA((2, lines)),
        ],
        compiler_params=pltpu.CompilerParams(vmem_limit_bytes=12 << 20),
        cost_estimate=cost,
        name="other_half",
    )(swapped, stored, own)


def per_device(activations, out_grads, project_in, project_out, lengths, stored_grads):
    slots = activations.shape[0] // lengths.shape[0]
    width = project_in.shape[1]
    plane = lax.axis_size(PLANE)
    lines = lax.axis_size("zl")

    def exchange(values, axes):
        return lax.all_to_all(values, axes, 0, 0, tiled=True)

    partial, scale = project(
        lengths, project_in.T, project_out.T, activations, out_grads, slots
    )
    partial = exchange(partial, PLANE)
    halves = scaled_sum(partial, scale, 2 * lines, width)
    halves = exchange(halves, LINE)
    queries = outer_products(halves, plane, slots, width)
    gathered = exchange(queries, PLANE)
    swapped = lax.ppermute(gathered, "c", [(0, 1), (1, 0)])
    scores = scores_of(gathered, swapped, stored_grads, lines)
    return scores.reshape(-1, stored_grads.shape[0])


def solution(mesh):
    fine = Mesh(mesh.devices.reshape(4, 4, 2, 4, 2), ("y", "x", "zh", "zl", "c"))
    feat, lane = ("y", "x", "zh"), ("zl", "c")
    placed = (
        P(lane, feat),
        P(lane, feat),
        P(feat, None),
        P(feat, None),
        P(lane),
        P(feat + lane, None),
    )
    return jax.shard_map(
        per_device, mesh=fine, in_specs=placed, out_specs=P(None, feat + lane), check_vma=False
    )
```
